32 devices in a mesh: frame: 4 (over y, x), height: 2 (over core), width: 4 (over z).
Axes of the slice: x: 2, y: 2, z: 4, core: 2. Of those that a mesh axis runs over, the one named last changes fastest.
Arguments:
- tokens: bfloat16 [4, 16, 8, 16, 1536], P('frame', None, 'height', 'width'), may hold values from -6 to 6
- qkv_weight: bfloat16 [3, 768, 1536], P(None, ('frame', 'height')), may hold values from -0.15625 to 0.15625
- tile_mask: int32 [4, 4, 2, 4], P('frame'), may hold values 0 or 1
Outputs:
- attended: bfloat16 [4, 16, 8, 16, 768], P('frame', None, 'height', 'width')
The draws below stay inside these ranges and needn't reach their ends.
Inputs may be any that keep to these rules, and one draw needn't show every extreme that they name: `tile_mask`: selection flag of each tile.
All inputs are finite; a program needn't handle non-finite values. No bound on the sum of `tile_mask` on one device may be relied on, other than what follows from the above.
Results may differ from the reference program's by a relative error of at most 0.0082.
Values may be sent and summed in bfloat16 or wider, within the bound.
A program may use at most 64 MiB of HBM per device.

```python
import jax
import jax.numpy as jnp
from jax import lax

D = 1536
HEADS = 6
HEAD_DIM = 128
TILE = 4
FT = 4
HW = 768
CLIPS = 4
NF = 16
NH = 8
NW = 16


def plant(values, key, low, largest):
    index_at = [jax.random.randint(jax.random.fold_in(key, axis), (), 0, length) for axis, length in enumerate(values.shape)]
    main_axis = values.shape.index(max(values.shape))
    next_to = index_at[:main_axis] + [(index_at[main_axis] + 1) % values.shape[main_axis]] + index_at[main_axis + 1:]
    return values.at[tuple(index_at)].set(low).at[tuple(next_to)].set(largest)


def block_levels(rng, extent, pieces, smallest, largest):
    factor_of = 1.0
    for position, shards_of in pieces:
        draws = jax.random.uniform(jax.random.fold_in(jax.random.fold_in(rng, 6), position), (shards_of,), jnp.float32, smallest / len(pieces), largest / len(pieces))
        factor_of = factor_of * jnp.repeat(jnp.exp(draws), extent[position] // shards_of).reshape((-1,) + (1,) * (len(extent) - 1 - position))
    return factor_of


def normal_values(stream_key, dims, scale, limit, shards=(), kind=jnp.bfloat16):
    array = jax.random.normal(stream_key, dims, jnp.float32) * scale
    if len(shards) > 0:
        array = block_levels(stream_key, dims, shards, -0.22, 0.18) * array
    return jnp.clip(array, min=-limit, max=limit).astype(kind)


def setup_inputs(seed: int = 0) -> dict:
    key_list = jax.random.split(jax.random.key(seed), 4)
    return {
        "tokens": normal_values(key_list[0], (CLIPS, NF, NH, NW, D), 1.0, 6.0, ((0, 4), (2, 2), (3, 4))),
        "qkv_weight": normal_values(key_list[1], (3, HW, D), D ** -0.5, 0.15625, ((1, 8),)),
        "tile_mask": plant((jax.random.randint(key_list[2], (CLIPS, FT, NH // TILE, NW // TILE), 0, 4) < 3).astype(jnp.int32), jax.random.fold_in(key_list[2], 1), 0, 1),
    }


epsilon = 1e-06

def project_line(line_tokens, weight_wide):
    values_wide = line_tokens.astype(jnp.float32)
    normed = values_wide * lax.rsqrt(lax.optimization_barrier(jnp.mean(values_wide * values_wide, -1, keepdims=True)) + epsilon)
    normed = lax.optimization_barrier(normed.astype(jnp.bfloat16)).astype(jnp.float32)
    raw = jnp.einsum('td,shd->sth', normed, weight_wide)
    line_count = line_tokens.shape[0]
    head_view = raw[:2].reshape(2, line_count, HEADS, HEAD_DIM)
    scaled = head_view * lax.rsqrt(lax.optimization_barrier(jnp.mean(head_view * head_view, -1, keepdims=True)) + epsilon)
    scaled = scaled.reshape(2, line_count, HEADS * HEAD_DIM)
    return jnp.concatenate([scaled, raw[2:]], 0).astype(jnp.bfloat16)

def one_clip(clip_tokens, clip_mask, weight_wide):
    tiles_frame = NF // TILE
    tiles_height = NH // TILE
    tiles_width = NW // TILE
    cube = TILE * TILE * TILE
    lines = clip_tokens.reshape(NF * NH, NW, D)
    projected = lax.map(lambda line_tokens: project_line(line_tokens, weight_wide), lines)
    projected = jnp.transpose(projected, (1, 0, 2, 3)).reshape(3, NF, NH, NW, HW)
    tiled = projected.reshape(3, tiles_frame, TILE, tiles_height, TILE, tiles_width, TILE, HW)
    tiled = jnp.transpose(tiled, (0, 1, 3, 5, 2, 4, 6, 7)).reshape(3, tiles_frame, tiles_height, tiles_width, cube, HW)
    query_tiles = tiled[0]
    pad_spec = ((1, 1), (1, 1), (1, 1), (0, 0), (0, 0))
    key_tiles = jnp.pad(tiled[1], pad_spec)
    value_tiles = jnp.pad(tiled[2], pad_spec)
    mask_padded = jnp.pad(clip_mask, 1)
    zero_index = jnp.zeros((), jnp.int32)

    def window_block(source, frame_tile, height_tile):
        slab_tiles = lax.dynamic_slice(source, (frame_tile, height_tile, zero_index, zero_index, zero_index), (3, 3, tiles_width + 2, cube, HW))
        stacked = jnp.stack([slab_tiles[:, :, offset:offset + tiles_width] for offset in range(3)], 2)
        return jnp.moveaxis(stacked, 3, 0).reshape(tiles_width, 27 * cube, HW)

    def slab(slab_index):
        frame_tile = (slab_index // tiles_height).astype(jnp.int32)
        height_tile = (slab_index % tiles_height).astype(jnp.int32)
        key_block = window_block(key_tiles, frame_tile, height_tile)
        value_block = window_block(value_tiles, frame_tile, height_tile)
        mask_slab = lax.dynamic_slice(mask_padded, (frame_tile, height_tile, zero_index), (3, 3, tiles_width + 2))
        mask_stack = jnp.stack([mask_slab[:, :, offset:offset + tiles_width] for offset in range(3)], 2)
        mask_rows = jnp.moveaxis(mask_stack, 3, 0).reshape(tiles_width, 27)
        allowed = (mask_rows == 1) | (jnp.arange(27) == 13)[None, :]
        allowed = jnp.repeat(allowed, cube, axis=1)
        query_block = lax.dynamic_slice(query_tiles, (frame_tile, height_tile, zero_index, zero_index, zero_index), (1, 1, tiles_width, cube, HW))[0, 0]
        query_heads = query_block.astype(jnp.float32).reshape(tiles_width, cube, HEADS, HEAD_DIM)
        key_heads = key_block.astype(jnp.float32).reshape(tiles_width, 27 * cube, HEADS, HEAD_DIM)
        value_heads = value_block.astype(jnp.float32).reshape(tiles_width, 27 * cube, HEADS, HEAD_DIM)
        scores = jnp.einsum('cqhd,ckhd->chqk', query_heads, key_heads) * HEAD_DIM ** (-0.5)
        weight = jnp.where(allowed[:, None, None, :], jnp.exp(scores), jnp.float32(0.0))
        total = lax.optimization_barrier(jnp.sum(weight, -1))
        rounded = lax.optimization_barrier(weight.astype(jnp.bfloat16)).astype(jnp.float32)
        summed = jnp.einsum('chqk,ckhd->cqhd', rounded, value_heads)
        result = summed / jnp.moveaxis(total, 1, 2)[..., None]
        return result.reshape(tiles_width, cube, HW).astype(jnp.bfloat16)
    slabs = lax.map(slab, jnp.arange(tiles_frame * tiles_height, dtype=jnp.int32))
    attended = slabs.reshape(tiles_frame, tiles_height, tiles_width, TILE, TILE, TILE, HW)
    attended = jnp.transpose(attended, (0, 3, 1, 4, 2, 5, 6)).reshape(NF, NH, NW, HW)
    return attended

def reference(tokens, qkv_weight, tile_mask):
    weight_wide = qkv_weight.astype(jnp.float32)
    return lax.map(lambda pair: one_clip(pair[0], pair[1], weight_wide), (tokens, tile_mask))
```

```python
import functools
import math

import jax
import jax.numpy as jnp
from jax import lax
from jax.experimental import pallas as pl
from jax.experimental.pallas import tpu as pltpu
from jax.sharding import PartitionSpec as P

HEAD_DIM = 128
TILE = 4
CUBE = TILE * TILE * TILE
MESH = pl.DeviceIdType.MESH

epsilon = 1e-06


def kernel(
    n_h, n_w, x_ref, w_ref, tm_ref, o_ref,
    xs, xn, w_all, kbuf, vbuf, qbuf, mask,
    loc_sem, tok_s, tok_r, own_s, own_r, fwd_s, fwd_r, hgt_s, hgt_r, kvx_s, kvx_r,
):
    f, h, w = lax.axis_index("frame"), lax.axis_index("height"), lax.axis_index("width")
    f1 = f + 1 - 2 * (f % 2)
    f2 = f + 2 - 4 * ((f // 2) % 2)
    rows = w_ref.shape[1]
    features = w_ref.shape[2]
    half = features // 2
    tokens = xn.shape[0] // 3
    heads = kbuf.shape[2]
    slots = kbuf.shape[1]
    key, value, query = 1, 2, 0

    def row(parity, height):
        return pl.ds(pl.multiple_of((parity * n_h + height) * rows, rows), rows)

    parity = f % 2
    mine, beside = row(parity, h), row(1 - parity, h)

    def remote(src, dst, send, recv, target):
        return pltpu.make_async_remote_copy(
            src_ref=src, dst_ref=dst, send_sem=send, recv_sem=recv,
            device_id=target, device_id_type=MESH,
        )

    def to_frame(i):
        return ((f1, f2)[i], h, w)

    def own_copy(s, i):
        return remote(w_ref.at[s], w_all.at[s, i, mine], own_s.at[s, i], own_r.at[s, i], to_frame(i))

    def fwd_copy(s, i):
        cols = pl.ds(0, half) if i == 1 else pl.ds(half, half)
        src = w_all.at[s, 0, beside, cols] if i == 1 else w_all.at[s, 1, mine, cols]
        dst = w_all.at[s, 1, beside if i == 1 else mine, cols]
        return remote(src, dst, fwd_s.at[s, i], fwd_r.at[s, i], to_frame(i))

    piece_at = ((0, mine), (0, beside), (1, mine), (1, beside))

    def hgt_copy(s, piece, d):
        group, place = piece_at[piece]
        dst = w_all.at[s, group, place]
        src = w_ref.at[s] if piece == 0 else dst
        target = (f, lax.rem(h + d, n_h), w)
        return remote(src, dst, hgt_s.at[s, piece, d - 1], hgt_r.at[s, piece, d - 1], target)

    def kv_copy(g, which, up):
        buf = (kbuf, vbuf)[which]
        slot = 1 if up or n_h == 2 else 2
        target = (f, h + 1 if up else h - 1, w)
        e = 0 if up else 1
        return remote(buf.at[g, 0], buf.at[g, slot], kvx_s.at[g, which, e], kvx_r.at[g, which, e], target)

    def tok_copy(e):
        target = (f, h, w + 1 if e == 0 else w - 1)
        return remote(x_ref.at[0], xs.at[0 if e == 0 else 2], tok_s.at[e], tok_r.at[e], target)

    local_x = pltpu.make_async_copy(x_ref.at[0], xs.at[1], loc_sem.at[0])
    local_w = [
        pltpu.make_async_copy(w_ref.at[s], w_all.at[s, 0, mine], loc_sem.at[1 + s]) for s in range(3)
    ]
    local_x.start()
    for s in range(3):
        local_w[s].start()

    has_left, has_right = w > 0, w < n_w - 1
    has_below, has_above = h > 0, h < n_h - 1

    barrier = pltpu.get_barrier_semaphore()

    def greet(target):
        pl.semaphore_signal(barrier, inc=1, device_id=target, device_id_type=MESH)

    greet(to_frame(0))
    greet(to_frame(1))
    for d in range(1, n_h):
        greet((f, lax.rem(h + d, n_h), w))

    @pl.when(has_left)
    def _():
        greet((f, h, w - 1))

    @pl.when(has_right)
    def _():
        greet((f, h, w + 1))

    peers = n_h + 1 + has_left.astype(jnp.int32) + has_right.astype(jnp.int32)
    pl.semaphore_wait(barrier, peers)

    for s in (key, value, query):
        own_copy(s, 0).start()
        own_copy(s, 1).start()
        if s == key:
            @pl.when(has_right)
            def _():
                tok_copy(0).start()

            @pl.when(has_left)
            def _():
                tok_copy(1).start()
        for d in range(1, n_h):
            hgt_copy(s, 0, d).start()

    q_tile = lax.broadcasted_iota(jnp.int32, (tokens, tokens), 0) // CUBE
    k_tile = lax.broadcasted_iota(jnp.int32, (tokens, tokens), 1) // CUBE
    near = jnp.abs(q_tile - k_tile) <= 1
    same = q_tile == k_tile
    total_h, total_w = tm_ref.shape[2], tm_ref.shape[3]
    for b in range(slots):
        if b == 0:
            row_h = h
        elif n_h == 2:
            row_h = 1 - h
        else:
            row_h = h - 1 if b == 1 else h + 1
        for c in range(3):
            col_w = w + c - 1
            inside = ((row_h >= 0) & (row_h < total_h) & (col_w >= 0) & (col_w < total_w)).astype(jnp.int32)
            at_h = jnp.minimum(jnp.maximum(row_h, 0), total_h - 1)
            at_w = jnp.minimum(jnp.maximum(col_w, 0), total_w - 1)
            flags = jnp.zeros((tokens, tokens), jnp.int32)
            for t in range(tokens // CUBE):
                flag = tm_ref[0, t, at_h, at_w] * inside
                flags = jnp.where(k_tile == t, flag, flags)
            seen = flags == 1
            if b == 0 and c == 1:
                seen = seen | same
            allowed = jnp.where(near & seen, jnp.float32(1.0), jnp.float32(0.0))
            mask[b, :, c * tokens : (c + 1) * tokens] = allowed.astype(jnp.bfloat16)

    def normalise(c):
        step = 64
        for t in range(tokens // step):
            frames = step // (TILE * TILE)
            block = xs[c, t * frames : (t + 1) * frames].astype(jnp.float32).reshape(step, features)
            scale = lax.rsqrt(jnp.mean(block * block, -1, keepdims=True) + epsilon)
            xn[c * tokens + t * step : c * tokens + (t + 1) * step, :] = (block * scale).astype(jnp.bfloat16)

    def blank(c):
        xn[c * tokens : (c + 1) * tokens, :] = jnp.zeros((tokens, features), jnp.bfloat16)

    local_x.wait()
    normalise(1)

    def relay(s):
        own_copy(s, 0).wait_recv()
        fwd_copy(s, 1).start()
        for d in range(1, n_h):
            hgt_copy(s, 1, d).start()
        own_copy(s, 1).wait_recv()
        fwd_copy(s, 0).start()
        for d in range(1, n_h):
            hgt_copy(s, 2, d).start()

    def head_norm(raw):
        return (raw * lax.rsqrt(jnp.mean(raw * raw, -1, keepdims=True) + epsilon)).astype(jnp.bfloat16)

    contract_last = (((1,), (1,)), ((), ()))

    def project_kv(g, s):
        buf = kbuf if s == key else vbuf

        def body(c, carry):
            at = pl.ds(pl.multiple_of(c * tokens, tokens), tokens)
            raw = lax.dot_general(xn[at, :], w_all[s, g], contract_last, preferred_element_type=jnp.float32)
            for j in range(heads):
                part = raw[:, j * HEAD_DIM : (j + 1) * HEAD_DIM]
                buf[g, 0, j, at, :] = head_norm(part) if s == key else part.astype(jnp.bfloat16)
            return carry

        lax.fori_loop(0, 3, body, 0)
        which = 0 if s == key else 1

        @pl.when(has_above)
        def _():
            kv_copy(g, which, True).start()

        @pl.when(has_below)
        def _():
            kv_copy(g, which, False).start()

    def project_q(g):
        raw = lax.dot_general(
            xn[tokens : 2 * tokens, :], w_all[query, g], contract_last, preferred_element_type=jnp.float32
        )
        for j in range(heads):
            qbuf[g, j] = head_norm(raw[:, j * HEAD_DIM : (j + 1) * HEAD_DIM])

    def wait_kv(g):
        for which in range(2):
            @pl.when(has_below)
            def _():
                kv_copy(g, which, True).wait_recv()

            @pl.when(has_above)
            def _():
                kv_copy(g, which, False).wait_recv()

    def wait_hgt(s, pieces):
        for piece in pieces:
            for d in range(1, n_h):
                hgt_copy(s, piece, d).wait_recv()

    factor = HEAD_DIM ** (-0.5) * math.log2(math.e)
    ones = jnp.ones((3 * tokens, HEAD_DIM), jnp.bfloat16)

    def attend(g):
        pair = f // 2
        base = (pair if g == 0 else 1 - pair) * heads

        def body(j, carry):
            q = qbuf[g, j]
            total = jnp.zeros((tokens, 2 * HEAD_DIM), jnp.float32)
            for b in range(slots):
                scores = lax.dot_general(q, kbuf[g, b, j], contract_last, preferred_element_type=jnp.float32)
                weight = jnp.exp2(scores * factor).astype(jnp.bfloat16) * mask[b]
                wide = jnp.concatenate([vbuf[g, b, j], ones], 1)
                total = total + jnp.dot(weight, wide, preferred_element_type=jnp.float32)
            result = (total[:, :HEAD_DIM] / total[:, HEAD_DIM:]).astype(o_ref.dtype)
            lanes = pl.ds(pl.multiple_of((base + j) * HEAD_DIM, HEAD_DIM), HEAD_DIM)
            o_ref[:, lanes] = result
            return carry

        lax.fori_loop(0, heads, body, 0)

    if n_h > 2:
        for edge, slot in ((h == 0, 1), (h == n_h - 1, 2)):
            @pl.when(edge)
            def _():
                for g in range(2):
                    kbuf[g, slot] = jnp.zeros(kbuf.shape[2:], jnp.bfloat16)
                    vbuf[g, slot] = jnp.zeros(vbuf.shape[2:], jnp.bfloat16)

    relay(key)
    relay(value)

    @pl.when(has_left)
    def _():
        tok_copy(0).wait_recv()
        normalise(0)

    @pl.when(w == 0)
    def _():
        blank(0)

    @pl.when(has_right)
    def _():
        tok_copy(1).wait_recv()
        normalise(2)

    @pl.when(w == n_w - 1)
    def _():
        blank(2)

    for s in (key, value):
        local_w[s].wait()
        wait_hgt(s, (0, 1))
        project_kv(0, s)
    relay(query)
    local_w[query].wait()
    wait_hgt(query, (0, 1))
    project_q(0)
    wait_kv(0)
    attend(0)
    for s in (key, value, query):
        fwd_copy(s, 0).wait_recv()
        fwd_copy(s, 1).wait_recv()
        for d in range(1, n_h):
            hgt_copy(s, 3, d).start()
        wait_hgt(s, (2, 3))
        if s == query:
            project_q(1)
        else:
            project_kv(1, s)
    wait_kv(1)
    attend(1)

    for s in range(3):
        for i in range(2):
            own_copy(s, i).wait_send()
            fwd_copy(s, i).wait_send()
        for piece in range(4):
            for d in range(1, n_h):
                hgt_copy(s, piece, d).wait_send()

    @pl.when(has_right)
    def _():
        tok_copy(0).wait_send()

    @pl.when(has_left)
    def _():
        tok_copy(1).wait_send()

    for g in range(2):
        for which in range(2):
            @pl.when(has_above)
            def _():
                kv_copy(g, which, True).wait_send()

            @pl.when(has_below)
            def _():
                kv_copy(g, which, False).wait_send()


def per_device(n_f, n_h, n_w, tokens, qkv_weight, tile_mask):
    clips, frames, rows, columns, features = tokens.shape
    count = frames * rows * columns
    width = qkv_weight.shape[1] * n_f * n_h
    if n_f != 4 or n_h < 2 or clips != 1 or rows != TILE or columns != TILE:
        raise ValueError("unsupported placement")
    heads = width // HEAD_DIM // 2
    slots = 2 if n_h == 2 else 3
    dma = pltpu.SemaphoreType.DMA
    out = pl.pallas_call(
        functools.partial(kernel, n_h, n_w),
        out_shape=jax.ShapeDtypeStruct((count, width), jnp.bfloat16),
        in_specs=[
            pl.BlockSpec(memory_space=pl.ANY),
            pl.BlockSpec(memory_space=pl.ANY),
            pl.BlockSpec(memory_space=pltpu.SMEM),
        ],
        out_specs=pl.BlockSpec(memory_space=pltpu.VMEM),
        scratch_shapes=[
            pltpu.VMEM((3, frames, rows, columns, features), jnp.bfloat16),
            pltpu.VMEM((3 * count, features), jnp.bfloat16),
            pltpu.VMEM((3, 2, width // 2, features), jnp.bfloat16),
            pltpu.VMEM((2, slots, heads, 3 * count, HEAD_DIM), jnp.bfloat16),
            pltpu.VMEM((2, slots, heads, 3 * count, HEAD_DIM), jnp.bfloat16),
            pltpu.VMEM((2, heads, count, HEAD_DIM), jnp.bfloat16),
            pltpu.VMEM((slots, count, 3 * count), jnp.bfloat16),
            dma((4,)), dma((2,)), dma((2,)), dma((3, 2)), dma((3, 2)), dma((3, 2)), dma((3, 2)),
            dma((3, 4, n_h - 1)), dma((3, 4, n_h - 1)), dma((2, 2, 2)), dma((2, 2, 2)),
        ],
        compiler_params=pltpu.CompilerParams(
            collective_id=0, has_side_effects=True, vmem_limit_bytes=56 << 20
        ),
    )(tokens, qkv_weight, tile_mask)
    return out.reshape(clips, frames, rows, columns, width)


def solution(mesh):
    in_specs = (
        P("frame", None, "height", "width", None),
        P(None, ("frame", "height"), None),
        P("frame", None, None, None),
    )
    out_specs = P("frame", None, "height", "width", None)
    body = functools.partial(
        per_device, mesh.shape["frame"], mesh.shape["height"], mesh.shape["width"]
    )
    return jax.shard_map(body, mesh=mesh, in_specs=in_specs, out_specs=out_specs, check_vma=False)
```

```python
import functools
import math

import jax
import jax.numpy as jnp
from jax import lax
from jax.experimental import pallas as pl
from jax.experimental.pallas import tpu as pltpu
from jax.sharding import PartitionSpec as P

HEAD_DIM = 128
TILE = 4
CUBE = TILE * TILE * TILE
MESH = pl.DeviceIdType.MESH

epsilon = 1e-06


def kernel(
    n_h, n_w, x_ref, w_ref, tm_ref, o_ref,
    xs, xn, w_all, kbuf, vbuf, qbuf, mask,
    loc_sem, tok_s, tok_r, own_s, own_r, fwd_s, fwd_r, hgt_s, hgt_r, kvx_s, kvx_r,
):
    f, h, w = lax.axis_index("frame"), lax.axis_index("height"), lax.axis_index("width")
    f1 = f + 1 - 2 * (f % 2)
    f2 = f + 2 - 4 * ((f // 2) % 2)
    rows = w_ref.shape[1]
    features = w_ref.shape[2]
    half = features // 2
    tokens = xn.shape[0] // 3
    heads = kbuf.shape[2]
    slots = kbuf.shape[1]
    key, value, query = 1, 2, 0

    def row(parity, height):
        return pl.ds(pl.multiple_of((parity * n_h + height) * rows, rows), rows)

    parity = f % 2
    mine, beside = row(parity, h), row(1 - parity, h)

    def remote(src, dst, send, recv, target):
        return pltpu.make_async_remote_copy(
            src_ref=src, dst_ref=dst, send_sem=send, recv_sem=recv,
            device_id=target, device_id_type=MESH,
        )

    def to_frame(i):
        return ((f1, f2)[i], h, w)

    def own_copy(s, p, i):
        cols = pl.ds(p * half, half)
        return remote(
            w_ref.at[s, :, cols], w_all.at[s, i, mine, cols], own_s.at[s, p, i], own_r.at[s, p, i], to_frame(i)
        )

    def fwd_copy(s, i):
        cols = pl.ds(0, half) if i == 1 else pl.ds(half, half)
        src = w_all.at[s, 0, beside, cols] if i == 1 else w_all.at[s, 1, mine, cols]
        dst = w_all.at[s, 1, beside if i == 1 else mine, cols]
        return remote(src, dst, fwd_s.at[s, i], fwd_r.at[s, i], to_frame(i))

    piece_at = ((0, mine), (0, beside), (1, mine), (1, beside))

    def hgt_copy(s, piece, d):
        group, place = piece_at[piece]
        dst = w_all.at[s, group, place]
        src = w_ref.at[s] if piece == 0 else dst
        target = (f, lax.rem(h + d, n_h), w)
        return remote(src, dst, hgt_s.at[s, piece, d - 1], hgt_r.at[s, piece, d - 1], target)

    def kv_copy(g, which, up):
        buf = (kbuf, vbuf)[which]
        slot = 1 if up or n_h == 2 else 2
        target = (f, h + 1 if up else h - 1, w)
        e = 0 if up else 1
        return remote(buf.at[g, 0], buf.at[g, slot], kvx_s.at[g, which, e], kvx_r.at[g, which, e], target)

    def tok_copy(e):
        target = (f, h, w + 1 if e == 0 else w - 1)
        return remote(x_ref.at[0], xs.at[0 if e == 0 else 2], tok_s.at[e], tok_r.at[e], target)

    local_x = pltpu.make_async_copy(x_ref.at[0], xs.at[1], loc_sem.at[0])
    local_w = [
        pltpu.make_async_copy(w_ref.at[s], w_all.at[s, 0, mine], loc_sem.at[1 + s]) for s in range(3)
    ]
    local_x.start()
    for s in range(3):
        local_w[s].start()

    has_left, has_right = w > 0, w < n_w - 1
    has_below, has_above = h > 0, h < n_h - 1

    barrier = pltpu.get_barrier_semaphore()

    def greet(target):
        pl.semaphore_signal(barrier, inc=1, device_id=target, device_id_type=MESH)

    greet(to_frame(0))
    greet(to_frame(1))
    for d in range(1, n_h):
        greet((f, lax.rem(h + d, n_h), w))

    @pl.when(has_left)
    def _():
        greet((f, h, w - 1))

    @pl.when(has_right)
    def _():
        greet((f, h, w + 1))

    peers = n_h + 1 + has_left.astype(jnp.int32) + has_right.astype(jnp.int32)
    pl.semaphore_wait(barrier, peers)

    def send_own(s, p):
        own_copy(s, p, 0).start()
        own_copy(s, p, 1).start()

    def wait_own(s, p):
        own_copy(s, p, 0).wait_recv()
        own_copy(s, p, 1).wait_recv()

    def send_fwd(s):
        fwd_copy(s, 0).start()
        fwd_copy(s, 1).start()

    def relay(s, *pieces):
        for piece in pieces:
            for d in range(1, n_h):
                hgt_copy(s, piece, d).start()

    def take_fwd(s):
        fwd_copy(s, 0).wait_recv()
        fwd_copy(s, 1).wait_recv()
        relay(s, 3)

    send_own(key, 0)
    send_own(key, 1)

    @pl.when(has_right)
    def _():
        tok_copy(0).start()

    @pl.when(has_left)
    def _():
        tok_copy(1).start()

    for s in (key, value, query):
        relay(s, 0)

    q_tile = lax.broadcasted_iota(jnp.int32, (tokens, tokens), 0) // CUBE
    k_tile = lax.broadcasted_iota(jnp.int32, (tokens, tokens), 1) // CUBE
    near = jnp.abs(q_tile - k_tile) <= 1
    same = q_tile == k_tile
    total_h, total_w = tm_ref.shape[2], tm_ref.shape[3]
    for b in range(slots):
        if b == 0:
            row_h = h
        elif n_h == 2:
            row_h = 1 - h
        else:
            row_h = h - 1 if b == 1 else h + 1
        for c in range(3):
            col_w = w + c - 1
            inside = ((row_h >= 0) & (row_h < total_h) & (col_w >= 0) & (col_w < total_w)).astype(jnp.int32)
            at_h = jnp.minimum(jnp.maximum(row_h, 0), total_h - 1)
            at_w = jnp.minimum(jnp.maximum(col_w, 0), total_w - 1)
            flags = jnp.zeros((tokens, tokens), jnp.int32)
            for t in range(tokens // CUBE):
                flag = tm_ref[0, t, at_h, at_w] * inside
                flags = jnp.where(k_tile == t, flag, flags)
            seen = flags == 1
            if b == 0 and c == 1:
                seen = seen | same
            allowed = jnp.where(near & seen, jnp.float32(1.0), jnp.float32(0.0))
            mask[b, :, c * tokens : (c + 1) * tokens] = allowed.astype(jnp.bfloat16)

    def normalise(c):
        step = 64
        for t in range(tokens // step):
            frames = step // (TILE * TILE)
            block = xs[c, t * frames : (t + 1) * frames].astype(jnp.float32).reshape(step, features)
            scale = lax.rsqrt(jnp.mean(block * block, -1, keepdims=True) + epsilon)
            xn[c * tokens + t * step : c * tokens + (t + 1) * step, :] = (block * scale).astype(jnp.bfloat16)

    def blank(c):
        xn[c * tokens : (c + 1) * tokens, :] = jnp.zeros((tokens, features), jnp.bfloat16)

    def head_norm(raw):
        return (raw * lax.rsqrt(jnp.mean(raw * raw, -1, keepdims=True) + epsilon)).astype(jnp.bfloat16)

    contract_last = (((1,), (1,)), ((), ()))

    def project_kv(g, s, sides):
        buf = kbuf if s == key else vbuf

        def block(c):
            at = pl.ds(pl.multiple_of(c * tokens, tokens), tokens)
            raw = lax.dot_general(xn[at, :], w_all[s, g], contract_last, preferred_element_type=jnp.float32)
            for j in range(heads):
                part = raw[:, j * HEAD_DIM : (j + 1) * HEAD_DIM]
                buf[g, 0, j, at, :] = head_norm(part) if s == key else part.astype(jnp.bfloat16)

        if not sides:
            block(1)
            return

        def body(i, carry):
            block(2 * i)
            return carry

        lax.fori_loop(0, 2, body, 0)
        which = 0 if s == key else 1

        @pl.when(has_above)
        def _():
            kv_copy(g, which, True).start()

        @pl.when(has_below)
        def _():
            kv_copy(g, which, False).start()

    def project_q(g, first, count):
        place = pl.ds(pl.multiple_of(first * HEAD_DIM, HEAD_DIM), count * HEAD_DIM)
        raw = lax.dot_general(
            xn[tokens : 2 * tokens, :], w_all[query, g, place], contract_last, preferred_element_type=jnp.float32
        )
        for j in range(count):
            qbuf[g, first + j] = head_norm(raw[:, j * HEAD_DIM : (j + 1) * HEAD_DIM])

    def wait_kv(g):
        for which in range(2):
            @pl.when(has_below)
            def _():
                kv_copy(g, which, True).wait_recv()

            @pl.when(has_above)
            def _():
                kv_copy(g, which, False).wait_recv()

    def wait_hgt(s, pieces):
        for piece in pieces:
            for d in range(1, n_h):
                hgt_copy(s, piece, d).wait_recv()

    factor = HEAD_DIM ** (-0.5) * math.log2(math.e)
    ones = jnp.ones((3 * tokens, HEAD_DIM), jnp.bfloat16)

    def attend(g, first, count):
        pair = f // 2
        base = (pair if g == 0 else 1 - pair) * heads

        def body(i, carry):
            j = first + i
            q = qbuf[g, j]
            total = jnp.zeros((tokens, 2 * HEAD_DIM), jnp.float32)
            for b in range(slots):
                scores = lax.dot_general(q, kbuf[g, b, j], contract_last, preferred_element_type=jnp.float32)
                weight = jnp.exp2(scores * factor).astype(jnp.bfloat16) * mask[b]
                wide = jnp.concatenate([vbuf[g, b, j], ones], 1)
                total = total + jnp.dot(weight, wide, preferred_element_type=jnp.float32)
            result = (total[:, :HEAD_DIM] / total[:, HEAD_DIM:]).astype(o_ref.dtype)
            lanes = pl.ds(pl.multiple_of((base + j) * HEAD_DIM, HEAD_DIM), HEAD_DIM)
            o_ref[:, lanes] = result
            return carry

        lax.fori_loop(0, count, body, 0)

    if n_h > 2:
        for edge, slot in ((h == 0, 1), (h == n_h - 1, 2)):
            @pl.when(edge)
            def _():
                for g in range(2):
                    kbuf[g, slot] = jnp.zeros(kbuf.shape[2:], jnp.bfloat16)
                    vbuf[g, slot] = jnp.zeros(vbuf.shape[2:], jnp.bfloat16)

    local_x.wait()
    normalise(1)
    wait_own(key, 0)
    send_own(value, 0)
    fwd_copy(key, 1).start()
    wait_own(key, 1)
    fwd_copy(key, 0).start()
    relay(key, 1, 2)
    wait_own(value, 0)
    send_own(value, 1)
    local_w[key].wait()
    wait_hgt(key, (0, 1))
    project_kv(0, key, False)
    take_fwd(key)
    send_own(query, 0)
    wait_hgt(key, (2, 3))
    project_kv(1, key, False)
    wait_own(value, 1)
    send_own(query, 1)
    relay(value, 1, 2)
    @pl.when(has_left)
    def _():
        tok_copy(0).wait_recv()
        normalise(0)

    @pl.when(w == 0)
    def _():
        blank(0)

    @pl.when(has_right)
    def _():
        tok_copy(1).wait_recv()
        normalise(2)

    @pl.when(w == n_w - 1)
    def _():
        blank(2)

    project_kv(0, key, True)
    wait_own(query, 0)
    send_fwd(value)
    local_w[value].wait()
    wait_hgt(value, (0, 1))
    project_kv(0, value, False)
    project_kv(0, value, True)
    wait_own(query, 1)
    send_fwd(query)
    relay(query, 1, 2)
    project_kv(1, key, True)
    early = n_h * rows // HEAD_DIM
    local_w[query].wait()
    wait_hgt(query, (0, 1))
    project_q(0, 0, heads)
    wait_hgt(query, (2,))
    project_q(1, parity * (heads - early), early)
    wait_kv(0)
    attend(0, 0, heads)
    take_fwd(value)
    wait_hgt(value, (2, 3))
    project_kv(1, value, False)
    project_kv(1, value, True)
    take_fwd(query)
    wait_kv(1)
    attend(1, parity * (heads - early), early)
    wait_hgt(query, (3,))
    project_q(1, (1 - parity) * early, heads - early)
    attend(1, (1 - parity) * early, heads - early)

    for s in range(3):
        for i in range(2):
            own_copy(s, 0, i).wait_send()
            own_copy(s, 1, i).wait_send()
            fwd_copy(s, i).wait_send()
        for piece in range(4):
            for d in range(1, n_h):
                hgt_copy(s, piece, d).wait_send()

    @pl.when(has_right)
    def _():
        tok_copy(0).wait_send()

    @pl.when(has_left)
    def _():
        tok_copy(1).wait_send()

    for g in range(2):
        for which in range(2):
            @pl.when(has_above)
            def _():
                kv_copy(g, which, True).wait_send()

            @pl.when(has_below)
            def _():
                kv_copy(g, which, False).wait_send()


def per_device(n_f, n_h, n_w, tokens, qkv_weight, tile_mask):
    clips, frames, rows, columns, features = tokens.shape
    count = frames * rows * columns
    width = qkv_weight.shape[1] * n_f * n_h
    if n_f != 4 or n_h < 2 or clips != 1 or rows != TILE or columns != TILE:
        raise ValueError("unsupported placement")
    heads = width // HEAD_DIM // 2
    slots = 2 if n_h == 2 else 3
    dma = pltpu.SemaphoreType.DMA
    out = pl.pallas_call(
        functools.partial(kernel, n_h, n_w),
        out_shape=jax.ShapeDtypeStruct((count, width), jnp.bfloat16),
        in_specs=[
            pl.BlockSpec(memory_space=pl.ANY),
            pl.BlockSpec(memory_space=pl.ANY),
            pl.BlockSpec(memory_space=pltpu.SMEM),
        ],
        out_specs=pl.BlockSpec(memory_space=pltpu.VMEM),
        scratch_shapes=[
            pltpu.VMEM((3, frames, rows, columns, features), jnp.bfloat16),
            pltpu.VMEM((3 * count, features), jnp.bfloat16),
            pltpu.VMEM((3, 2, width // 2, features), jnp.bfloat16),
            pltpu.VMEM((2, slots, heads, 3 * count, HEAD_DIM), jnp.bfloat16),
            pltpu.VMEM((2, slots, heads, 3 * count, HEAD_DIM), jnp.bfloat16),
            pltpu.VMEM((2, heads, count, HEAD_DIM), jnp.bfloat16),
            pltpu.VMEM((slots, count, 3 * count), jnp.bfloat16),
            dma((4,)), dma((2,)), dma((2,)), dma((3, 2, 2)), dma((3, 2, 2)), dma((3, 2)), dma((3, 2)),
            dma((3, 4, n_h - 1)), dma((3, 4, n_h - 1)), dma((2, 2, 2)), dma((2, 2, 2)),
        ],
        compiler_params=pltpu.CompilerParams(
            collective_id=0, has_side_effects=True, vmem_limit_bytes=56 << 20
        ),
    )(tokens, qkv_weight, tile_mask)
    return out.reshape(clips, frames, rows, columns, width)


def solution(mesh):
    in_specs = (
        P("frame", None, "height", "width", None),
        P(None, ("frame", "height"), None),
        P("frame", None, None, None),
    )
    out_specs = P("frame", None, "height", "width", None)
    body = functools.partial(
        per_device, mesh.shape["frame"], mesh.shape["height"], mesh.shape["width"]
    )
    return jax.shard_map(body, mesh=mesh, in_specs=in_specs, out_specs=out_specs, check_vma=False)
```

```python
import functools
import math

import jax
import jax.numpy as jnp
from jax import lax
from jax.experimental import pallas as pl
from jax.experimental.pallas import tpu as pltpu
from jax.sharding import PartitionSpec as P

HEAD_DIM = 128
TILE = 4
CUBE = TILE * TILE * TILE
MESH = pl.DeviceIdType.MESH

epsilon = 1e-06


def kernel(
    n_h, n_w, x_ref, w_ref, tm_ref, o_ref,
    xs, xn, w_all, kbuf, vbuf, qbuf, mask,
    loc_sem, tok_s, tok_r, own_s, own_r, fwd_s, fwd_r, hgt_s, hgt_r, kvx_s, kvx_r,
):
    f, h, w = lax.axis_index("frame"), lax.axis_index("height"), lax.axis_index("width")
    f1 = f + 1 - 2 * (f % 2)
    f2 = f + 2 - 4 * ((f // 2) % 2)
    rows = w_ref.shape[1]
    features = w_ref.shape[2]
    half = features // 2
    tokens = xn.shape[0] // 3
    heads = kbuf.shape[2]
    slots = kbuf.shape[1]
    key, value, query = 1, 2, 0

    def row(parity, height):
        return pl.ds(pl.multiple_of((parity * n_h + height) * rows, rows), rows)

    parity = f % 2
    mine, beside = row(parity, h), row(1 - parity, h)

    def remote(src, dst, send, recv, target):
        return pltpu.make_async_remote_copy(
            src_ref=src, dst_ref=dst, send_sem=send, recv_sem=recv,
            device_id=target, device_id_type=MESH,
        )

    def to_frame(i):
        return ((f1, f2)[i], h, w)

    def own_copy(s, p, i):
        cols = pl.ds(p * half, half)
        return remote(
            w_ref.at[s, :, cols], w_all.at[s, i, mine, cols], own_s.at[s, p, i], own_r.at[s, p, i], to_frame(i)
        )

    def fwd_copy(s, i):
        cols = pl.ds(0, half) if i == 1 else pl.ds(half, half)
        src = w_all.at[s, 0, beside, cols] if i == 1 else w_all.at[s, 1, mine, cols]
        dst = w_all.at[s, 1, beside if i == 1 else mine, cols]
        return remote(src, dst, fwd_s.at[s, i], fwd_r.at[s, i], to_frame(i))

    piece_at = ((0, mine), (0, beside), (1, mine), (1, beside))

    def hgt_copy(s, piece, d):
        group, place = piece_at[piece]
        dst = w_all.at[s, group, place]
        src = w_ref.at[s] if piece == 0 else dst
        target = (f, lax.rem(h + d, n_h), w)
        return remote(src, dst, hgt_s.at[s, piece, d - 1], hgt_r.at[s, piece, d - 1], target)

    def kv_copy(g, which, up):
        buf = (kbuf, vbuf)[which]
        slot = 1 if up or n_h == 2 else 2
        target = (f, h + 1 if up else h - 1, w)
        e = 0 if up else 1
        return remote(buf.at[g, 0], buf.at[g, slot], kvx_s.at[g, which, e], kvx_r.at[g, which, e], target)

    def tok_copy(e):
        target = (f, h, w + 1 if e == 0 else w - 1)
        return remote(x_ref.at[0], xs.at[1 if e == 0 else 2], tok_s.at[e], tok_r.at[e], target)

    local_x = pltpu.make_async_copy(x_ref.at[0], xs.at[0], loc_sem.at[0])
    local_w = [
        pltpu.make_async_copy(w_ref.at[s], w_all.at[s, 0, mine], loc_sem.at[1 + s]) for s in range(3)
    ]
    local_x.start()
    for s in range(3):
        local_w[s].start()

    has_left, has_right = w > 0, w < n_w - 1
    has_below, has_above = h > 0, h < n_h - 1

    barrier = pltpu.get_barrier_semaphore()

    def greet(target):
        pl.semaphore_signal(barrier, inc=1, device_id=target, device_id_type=MESH)

    greet(to_frame(0))
    greet(to_frame(1))
    for d in range(1, n_h):
        greet((f, lax.rem(h + d, n_h), w))

    @pl.when(has_left)
    def _():
        greet((f, h, w - 1))

    @pl.when(has_right)
    def _():
        greet((f, h, w + 1))

    peers = n_h + 1 + has_left.astype(jnp.int32) + has_right.astype(jnp.int32)
    pl.semaphore_wait(barrier, peers)

    def send_own(s, p):
        own_copy(s, p, 0).start()
        own_copy(s, p, 1).start()

    def wait_own(s, p):
        own_copy(s, p, 0).wait_recv()
        own_copy(s, p, 1).wait_recv()

    def send_fwd(s):
        fwd_copy(s, 0).start()
        fwd_copy(s, 1).start()

    def relay(s, *pieces):
        for piece in pieces:
            for d in range(1, n_h):
                hgt_copy(s, piece, d).start()

    def take_fwd(s):
        fwd_copy(s, 0).wait_recv()
        fwd_copy(s, 1).wait_recv()
        relay(s, 3)

    send_own(key, 0)
    send_own(key, 1)

    @pl.when(has_right)
    def _():
        tok_copy(0).start()

    @pl.when(has_left)
    def _():
        tok_copy(1).start()

    for s in (key, value, query):
        relay(s, 0)

    q_tile = lax.broadcasted_iota(jnp.int32, (tokens, tokens), 0) // CUBE
    k_tile = lax.broadcasted_iota(jnp.int32, (tokens, tokens), 1) // CUBE
    near = jnp.abs(q_tile - k_tile) <= 1
    same = q_tile == k_tile
    total_h, total_w = tm_ref.shape[2], tm_ref.shape[3]
    for b in range(slots):
        if b == 0:
            row_h = h
        elif n_h == 2:
            row_h = 1 - h
        else:
            row_h = h - 1 if b == 1 else h + 1
        for c in range(3):
            col_w = w + (0, -1, 1)[c]
            inside = ((row_h >= 0) & (row_h < total_h) & (col_w >= 0) & (col_w < total_w)).astype(jnp.int32)
            at_h = jnp.minimum(jnp.maximum(row_h, 0), total_h - 1)
            at_w = jnp.minimum(jnp.maximum(col_w, 0), total_w - 1)
            flags = jnp.zeros((tokens, tokens), jnp.int32)
            for t in range(tokens // CUBE):
                flag = tm_ref[0, t, at_h, at_w] * inside
                flags = jnp.where(k_tile == t, flag, flags)
            seen = flags == 1
            if b == 0 and c == 0:
                seen = seen | same
            allowed = jnp.where(near & seen, jnp.float32(1.0), jnp.float32(0.0))
            mask[b, :, c * tokens : (c + 1) * tokens] = allowed.astype(jnp.bfloat16)

    def normalise(c):
        step = 64
        for t in range(tokens // step):
            frames = step // (TILE * TILE)
            block = xs[c, t * frames : (t + 1) * frames].astype(jnp.float32).reshape(step, features)
            scale = lax.rsqrt(jnp.mean(block * block, -1, keepdims=True) + epsilon)
            xn[c * tokens + t * step : c * tokens + (t + 1) * step, :] = (block * scale).astype(jnp.bfloat16)

    def blank(c):
        xn[c * tokens : (c + 1) * tokens, :] = jnp.zeros((tokens, features), jnp.bfloat16)

    def head_norm(raw):
        return (raw * lax.rsqrt(jnp.mean(raw * raw, -1, keepdims=True) + epsilon)).astype(jnp.bfloat16)

    contract_last = (((1,), (1,)), ((), ()))

    def project_kv(g, s, sides):
        buf = kbuf if s == key else vbuf

        at = {0: pl.ds(0, tokens), 1: pl.ds(tokens, 2 * tokens), 2: pl.ds(0, 3 * tokens)}[sides]
        raw = lax.dot_general(xn[at, :], w_all[s, g], contract_last, preferred_element_type=jnp.float32)
        for j in range(heads):
            part = raw[:, j * HEAD_DIM : (j + 1) * HEAD_DIM]
            buf[g, 0, j, at, :] = head_norm(part) if s == key else part.astype(jnp.bfloat16)
        if not sides:
            return

        which = 0 if s == key else 1

        @pl.when(has_above)
        def _():
            kv_copy(g, which, True).start()

        @pl.when(has_below)
        def _():
            kv_copy(g, which, False).start()

    def project_q(g, first, count):
        place = pl.ds(pl.multiple_of(first * HEAD_DIM, HEAD_DIM), count * HEAD_DIM)
        raw = lax.dot_general(
            xn[0:tokens, :], w_all[query, g, place], contract_last, preferred_element_type=jnp.float32
        )
        for j in range(count):
            qbuf[g, first + j] = head_norm(raw[:, j * HEAD_DIM : (j + 1) * HEAD_DIM])

    def wait_kv(g):
        for which in range(2):
            @pl.when(has_below)
            def _():
                kv_copy(g, which, True).wait_recv()

            @pl.when(has_above)
            def _():
                kv_copy(g, which, False).wait_recv()

    def wait_hgt(s, pieces):
        for piece in pieces:
            for d in range(1, n_h):
                hgt_copy(s, piece, d).wait_recv()

    factor = HEAD_DIM ** (-0.5) * math.log2(math.e)
    ones = jnp.ones((3 * tokens, HEAD_DIM), jnp.bfloat16)

    def attend(g, first, count):
        pair = f // 2
        base = (pair if g == 0 else 1 - pair) * heads

        def body(i, carry):
            j = first + i
            q = qbuf[g, j]
            total = jnp.zeros((tokens, 2 * HEAD_DIM), jnp.float32)
            for b in range(slots):
                scores = lax.dot_general(q, kbuf[g, b, j], contract_last, preferred_element_type=jnp.float32)
                weight = jnp.exp2(scores * factor).astype(jnp.bfloat16) * mask[b]
                wide = jnp.concatenate([vbuf[g, b, j], ones], 1)
                total = total + jnp.dot(weight, wide, preferred_element_type=jnp.float32)
            result = (total[:, :HEAD_DIM] / total[:, HEAD_DIM:]).astype(o_ref.dtype)
            lanes = pl.ds(pl.multiple_of((base + j) * HEAD_DIM, HEAD_DIM), HEAD_DIM)
            o_ref[:, lanes] = result
            return carry

        lax.fori_loop(0, count, body, 0)

    if n_h > 2:
        for edge, slot in ((h == 0, 1), (h == n_h - 1, 2)):
            @pl.when(edge)
            def _():
                for g in range(2):
                    kbuf[g, slot] = jnp.zeros(kbuf.shape[2:], jnp.bfloat16)
                    vbuf[g, slot] = jnp.zeros(vbuf.shape[2:], jnp.bfloat16)

    local_x.wait()
    normalise(0)
    wait_own(key, 0)
    send_own(value, 0)
    fwd_copy(key, 1).start()
    wait_own(key, 1)
    fwd_copy(key, 0).start()
    relay(key, 1, 2)
    wait_own(value, 0)
    send_own(value, 1)
    local_w[key].wait()
    wait_hgt(key, (0, 1))
    project_kv(0, key, 0)
    take_fwd(key)
    send_own(query, 0)
    wait_hgt(key, (2, 3))
    project_kv(1, key, 0)
    wait_own(value, 1)
    send_own(query, 1)
    relay(value, 1, 2)
    @pl.when(has_left)
    def _():
        tok_copy(0).wait_recv()
        normalise(1)

    @pl.when(w == 0)
    def _():
        blank(1)

    @pl.when(has_right)
    def _():
        tok_copy(1).wait_recv()
        normalise(2)

    @pl.when(w == n_w - 1)
    def _():
        blank(2)

    project_kv(0, key, 1)
    wait_own(query, 0)
    send_fwd(value)
    local_w[value].wait()
    wait_hgt(value, (0, 1))
    project_kv(0, value, 2)
    wait_own(query, 1)
    send_fwd(query)
    relay(query, 1, 2)
    project_kv(1, key, 1)
    early = n_h * rows // HEAD_DIM
    local_w[query].wait()
    wait_hgt(query, (0, 1))
    project_q(0, 0, heads)
    wait_hgt(query, (2,))
    project_q(1, parity * (heads - early), early)
    wait_kv(0)
    attend(0, 0, heads)
    take_fwd(value)
    wait_hgt(value, (2, 3))
    project_kv(1, value, 2)
    take_fwd(query)
    wait_kv(1)
    attend(1, parity * (heads - early), early)
    wait_hgt(query, (3,))
    project_q(1, (1 - parity) * early, heads - early)
    attend(1, (1 - parity) * early, heads - early)

    for s in range(3):
        for i in range(2):
            own_copy(s, 0, i).wait_send()
            own_copy(s, 1, i).wait_send()
            fwd_copy(s, i).wait_send()
        for piece in range(4):
            for d in range(1, n_h):
                hgt_copy(s, piece, d).wait_send()

    @pl.when(has_right)
    def _():
        tok_copy(0).wait_send()

    @pl.when(has_left)
    def _():
        tok_copy(1).wait_send()

    for g in range(2):
        for which in range(2):
            @pl.when(has_above)
            def _():
                kv_copy(g, which, True).wait_send()

            @pl.when(has_below)
            def _():
                kv_copy(g, which, False).wait_send()


def per_device(n_f, n_h, n_w, tokens, qkv_weight, tile_mask):
    clips, frames, rows, columns, features = tokens.shape
    count = frames * rows * columns
    width = qkv_weight.shape[1] * n_f * n_h
    if n_f != 4 or n_h < 2 or clips != 1 or rows != TILE or columns != TILE:
        raise ValueError("unsupported placement")
    heads = width // HEAD_DIM // 2
    slots = 2 if n_h == 2 else 3
    dma = pltpu.SemaphoreType.DMA
    out = pl.pallas_call(
        functools.partial(kernel, n_h, n_w),
        out_shape=jax.ShapeDtypeStruct((count, width), jnp.bfloat16),
        in_specs=[
            pl.BlockSpec(memory_space=pl.ANY),
            pl.BlockSpec(memory_space=pl.ANY),
            pl.BlockSpec(memory_space=pltpu.SMEM),
        ],
        out_specs=pl.BlockSpec(memory_space=pltpu.VMEM),
        scratch_shapes=[
            pltpu.VMEM((3, frames, rows, columns, features), jnp.bfloat16),
            pltpu.VMEM((3 * count, features), jnp.bfloat16),
            pltpu.VMEM((3, 2, width // 2, features), jnp.bfloat16),
            pltpu.VMEM((2, slots, heads, 3 * count, HEAD_DIM), jnp.bfloat16),
            pltpu.VMEM((2, slots, heads, 3 * count, HEAD_DIM), jnp.bfloat16),
            pltpu.VMEM((2, heads, count, HEAD_DIM), jnp.bfloat16),
            pltpu.VMEM((slots, count, 3 * count), jnp.bfloat16),
            dma((4,)), dma((2,)), dma((2,)), dma((3, 2, 2)), dma((3, 2, 2)), dma((3, 2)), dma((3, 2)),
            dma((3, 4, n_h - 1)), dma((3, 4, n_h - 1)), dma((2, 2, 2)), dma((2, 2, 2)),
        ],
        compiler_params=pltpu.CompilerParams(
            collective_id=0, has_side_effects=True, vmem_limit_bytes=56 << 20
        ),
    )(tokens, qkv_weight, tile_mask)
    return out.reshape(clips, frames, rows, columns, width)


def solution(mesh):
    in_specs = (
        P("frame", None, "height", "width", None),
        P(None, ("frame", "height"), None),
        P("frame", None, None, None),
    )
    out_specs = P("frame", None, "height", "width", None)
    body = functools.partial(
        per_device, mesh.shape["frame"], mesh.shape["height"], mesh.shape["width"]
    )
    return jax.shard_map(body, mesh=mesh, in_specs=in_specs, out_specs=out_specs, check_vma=False)
```
